256 devices in a mesh: freq: 8 (over z), space: 32 (over y, x, core).
Axes of the slice: x: 4, y: 4, z: 8, core: 2. Of those that a mesh axis runs over, the one named last changes fastest.
Arguments:
- direct: bfloat16 [2, 512, 262144], P(None, 'freq', 'space'), may hold values from -6 to 6
- adjoint: bfloat16 [2, 512, 262144], P(None, 'freq', 'space'), may hold values from -1.5258789e-05 to 1.5258789e-05
- coupling: float32 [7, 262144], P(None, 'space'), may hold values from 0.25 to 2
- wall: int32 [262144], P('space'), may hold values 0 or 1
Outputs:
- modes: bfloat16 [2, 512, 262144], P(None, 'freq', 'space')
- reduced: float32 [2, 512, 512], replicated
The draws below stay inside these ranges and needn't reach their ends.
All inputs are finite; a program needn't handle non-finite values. No bound on the sum of `wall` on one device may be relied on, other than what follows from the above.
Results may differ from the reference program's by a relative error of at most 0.007.
Values may be sent and summed in bfloat16 or wider, within the bound.
No kernel may reach another device: no remote copies, remote signals or barrier semaphores. Data moves between devices by JAX's collectives and lax.ppermute only.
A program may use at most 64 MiB of HBM per device.

```python
import jax
import jax.numpy as jnp
from jax import lax

COLS = 512
NY = 64
NZ = 64
ITERS = 2
NCELL = 262144


def place_ends(entries, own_key, smallest, top_value):
    dims = entries.shape
    index_at = [jax.random.randint(jax.random.fold_in(own_key, axis), (), 0, dims[axis]) for axis in range(len(dims))]
    entries = entries.at[tuple(index_at)].set(smallest)
    longest = dims.index(max(dims))
    index_at[longest] = (index_at[longest] + 1) % dims[longest]
    return entries.at[tuple(index_at)].set(top_value)


def level_of(own_key, dims, pieces, smallest, largest):
    level = 1.0
    for axis_at, shards_of in pieces:
        draws = jax.random.uniform(jax.random.fold_in(jax.random.fold_in(own_key, 6), axis_at), (shards_of,), jnp.float32, smallest / len(pieces), largest / len(pieces))
        level = level * jnp.repeat(jnp.exp(draws), dims[axis_at] // shards_of).reshape((-1,) + (1,) * (len(dims) - 1 - axis_at))
    return level


def scatter_about(stream_key, dims, spread, limit, split=(), kind=jnp.bfloat16):
    entries = jax.random.normal(stream_key, dims, jnp.float32) * spread
    if len(split) > 0:
        entries = level_of(stream_key, dims, split, -0.22, 0.18) * entries
    return jnp.clip(entries, min=-limit, max=limit).astype(kind)


def setup_inputs(seed: int = 0) -> dict:
    splits = jax.random.split(jax.random.key(seed), 5)
    direct = scatter_about(splits[0], (2, COLS, NCELL), 1.0, 6.0, ((1, 8), (2, 32)))
    adjoint = scatter_about(splits[1], (2, COLS, NCELL), (2 * NCELL * COLS * COLS) ** -0.5, 1.52587890625e-05, ((1, 8), (2, 32)))
    coupling = jnp.clip(0.25 + 1.75 * jax.random.uniform(splits[2], (7, NCELL), jnp.float32) ** level_of(splits[2], (7, NCELL), ((1, 32),), -0.2, 0.2), 0.25, 2.0)
    wall = place_ends((jax.random.randint(splits[3], (NCELL,), 0, 8) < 1).astype(jnp.int32), jax.random.fold_in(splits[3], 1), 0, 1)
    return {"direct": direct, "adjoint": adjoint, "coupling": coupling, "wall": wall}


def complex_product(left_re, left_im, right_re, right_im):
    highest = lax.Precision.HIGHEST
    out_re = jnp.dot(left_re, right_re, precision=highest) - jnp.dot(left_im, right_im, precision=highest)
    out_im = jnp.dot(left_re, right_im, precision=highest) + jnp.dot(left_im, right_re, precision=highest)
    return out_re, out_im


def newton_schulz(hank_re, hank_im):
    total = jnp.sum(hank_re * hank_re + hank_im * hank_im)
    factor = 2.0 / total
    inverse_re = factor * hank_re.T
    inverse_im = -factor * hank_im.T
    identity = jnp.eye(hank_re.shape[0], dtype=jnp.float32)
    for iteration in range(ITERS):
        prod_re, prod_im = complex_product(hank_re, hank_im, inverse_re, inverse_im)
        inverse_re, inverse_im = complex_product(inverse_re, inverse_im, 2.0 * identity - prod_re, -prod_im)
    return inverse_re, inverse_im


def apply_operator(padded, coupling_local, wall_local, span_z):
    inner = padded[:, 1:-1]
    width = inner.shape[2]
    zero_rows = jnp.zeros(inner.shape[:2] + (span_z,), inner.dtype)
    zero_one = zero_rows[:, :, :1]
    north = jnp.concatenate([inner[:, :, span_z:], zero_rows], 2)
    south = jnp.concatenate([zero_rows, inner[:, :, :width - span_z]], 2)
    east = jnp.concatenate([inner[:, :, 1:], zero_one], 2)
    west = jnp.concatenate([zero_one, inner[:, :, :width - 1]], 2)
    zpos = jnp.arange(width, dtype=jnp.int32) % span_z
    east = jnp.where(zpos == span_z - 1, jnp.zeros_like(east), east)
    west = jnp.where(zpos == 0, jnp.zeros_like(west), west)
    beside = coupling_local[1] * padded[:, 2:] + coupling_local[2] * padded[:, :-2]
    beside = beside + coupling_local[3] * north + coupling_local[4] * south
    beside = beside + coupling_local[5] * east + coupling_local[6] * west
    result = coupling_local[0] * inner - beside
    return jnp.where(wall_local == 1, inner.astype(result.dtype), result)


def reference(direct, adjoint, coupling, wall):
    columns = direct.shape[1]
    ncells = direct.shape[2]
    plane = NY * NZ
    planes_all = ncells // plane
    adj_cat = jnp.concatenate([adjoint[0], adjoint[1]], 1)
    dir_stack = jnp.concatenate([jnp.concatenate([direct[0], direct[1]], 1), jnp.concatenate([direct[1], -direct[0]], 1)], 0)
    hank = lax.dot_general(adj_cat, dir_stack, (((1,), (1,)), ((), ())), preferred_element_type=jnp.float32)
    inverse_re, inverse_im = newton_schulz(hank[:, :columns], hank[:, columns:])
    bal_re = inverse_re.astype(jnp.bfloat16)
    bal_im = inverse_im.astype(jnp.bfloat16)
    mapping = jnp.concatenate([jnp.concatenate([bal_re.T, -bal_im.T], 1), jnp.concatenate([bal_im.T, bal_re.T], 1)], 0)
    phi = jnp.dot(mapping, jnp.concatenate([direct[0], direct[1]], 0), preferred_element_type=jnp.float32)
    modes = phi.astype(jnp.bfloat16).reshape(2, columns, ncells)
    field = phi.reshape(2 * columns, planes_all, plane)
    padded = jnp.pad(field, ((0, 0), (1, 1), (0, 0)))
    image = apply_operator(padded, coupling.reshape(7, planes_all, plane), wall.reshape(planes_all, plane), NZ)
    image = image.reshape(2, columns, ncells)
    img_stack = jnp.concatenate([jnp.concatenate([image[0], image[1]], 1), jnp.concatenate([image[1], -image[0]], 1)], 0)
    projected = lax.dot_general(adj_cat.astype(jnp.float32), img_stack, (((1,), (1,)), ((), ())), precision=lax.Precision.HIGHEST)
    scale_out = columns / 16.0
    reduced = scale_out * jnp.stack([projected[:, :columns], projected[:, columns:]], 0)
    return modes, reduced
```

```python
import functools

import jax
import jax.numpy as jnp
from jax import lax
from jax.experimental import pallas as pl
from jax.experimental.pallas import tpu as pltpu
from jax.sharding import PartitionSpec as P

NY = 64
NZ = 64
PLANE = NY * NZ
BF = jnp.bfloat16
F32 = jnp.float32
PARAMS = pltpu.CompilerParams(vmem_limit_bytes=56 * 1024 * 1024)
NT = (((1,), (1,)), ((), ()))
NN = (((1,), (0,)), ((), ()))


def call(kernel, outs, args, name, scratch=(), flops=0, moved=0):
    return pl.pallas_call(
        kernel,
        out_shape=outs,
        scratch_shapes=list(scratch),
        compiler_params=PARAMS,
        name=name,
        cost_estimate=pl.CostEstimate(flops=flops, bytes_accessed=moved, transcendentals=0),
    )(*args)


def spread_kernel(nf, chunk, x_ref, *refs):
    outs = refs[-nf:]
    me = lax.axis_index("freq")
    for d in range(nf):
        dest = lax.rem(me + d, nf)
        for p in range(2):
            at = pl.multiple_of(p * PLANE + dest * chunk, chunk)
            outs[d][:, :, p * chunk : (p + 1) * chunk] = x_ref[:, :, pl.ds(at, chunk)]


def spread(x, nf, after=()):
    chunk = PLANE // nf
    cols = x.shape[1]
    outs = [jax.ShapeDtypeStruct((2, cols, 2 * chunk), BF)] * nf
    specs = [pl.BlockSpec(memory_space=pltpu.VMEM)] + [pl.BlockSpec(memory_space=pl.ANY)] * len(after)
    return pl.pallas_call(
        functools.partial(spread_kernel, nf, chunk),
        out_shape=outs,
        in_specs=specs,
        compiler_params=PARAMS,
        name="spread",
        cost_estimate=pl.CostEstimate(flops=0, bytes_accessed=2 * x.size * 2, transcendentals=0),
    )(x, *after)


def rotate(parts, nf):
    got = [parts[0]]
    for d in range(1, nf):
        got.append(lax.ppermute(parts[d], "freq", [(i, (i + d) % nf) for i in range(nf)]))
    return got


def gather_kernel(nf, cols, chunk, *refs):
    parts = refs[:nf]
    full, low, high, first, last = refs[nf:]
    me = lax.axis_index("freq")
    for d in range(nf):
        src = lax.rem(me + nf - d, nf)
        at = pl.multiple_of(src * cols, cols)
        for c in range(2):
            block = parts[d][c]
            full[c, pl.ds(at, cols), :] = block
            low[c, pl.ds(at, cols), :] = block[:, :chunk]
            high[c, pl.ds(at, cols), :] = block[:, chunk:]
            a, b = block[:, :128].astype(F32), block[:, chunk : chunk + 128].astype(F32)
            first[c, pl.ds(at, cols), :] = jnp.concatenate([a[:, :NZ], b[:, :NZ]], 1).astype(BF)
            a, b = block[:, chunk - 128 : chunk].astype(F32), block[:, 2 * chunk - 128 :].astype(F32)
            last[c, pl.ds(at, cols), :] = jnp.concatenate([a[:, NZ:], b[:, NZ:]], 1).astype(BF)


def stencil_kernel(chunk, x_ref, up_ref, down_ref, north_ref, south_ref, e_ref, w_ref):
    per = chunk // 128
    rows = x_ref.shape[0]
    lane = lax.broadcasted_iota(jnp.int32, (rows, 128), 1)
    front = lane < NZ
    cells = lambda ref, j: ref[:, j * 128 : (j + 1) * 128].astype(F32)
    for p in range(2):
        north, south = north_ref[...].astype(F32), south_ref[...].astype(F32)
        if p == 0:
            north = pltpu.roll(north, NZ, 1)
        else:
            south = pltpu.roll(south, NZ, 1)
        turned = [south]
        for j in range(per):
            turned.append(pltpu.roll(cells(x_ref, p * per + j), NZ, 1))
        turned.append(north)
        for j in range(per):
            k = p * per + j
            x = cells(x_ref, k)
            ahead = cells(x_ref, per + j) if p == 0 else cells(up_ref, j)
            behind = cells(down_ref, j) if p == 0 else cells(x_ref, j)
            e = [e_ref[i : i + 1, k * 128 : (k + 1) * 128] for i in range(7)]
            beside = e[1] * ahead + e[2] * behind
            beside = beside + e[3] * jnp.where(front, turned[j + 1], turned[j + 2])
            beside = beside + e[4] * jnp.where(front, turned[j], turned[j + 1])
            beside = beside + e[5] * pltpu.roll(x, 127, 1) + e[6] * pltpu.roll(x, 1, 1)
            w_ref[:, k * 128 : (k + 1) * 128] = (e[0] * x - beside).astype(BF)


def stencil(full, up, down, north, south, coeff, chunk):
    rows = full.shape[0] * full.shape[1]
    step = 128
    flat = lambda v: v.reshape(rows, v.shape[2])
    spec = lambda width: pl.BlockSpec((step, width), lambda i: (i, 0))
    out = pl.pallas_call(
        functools.partial(stencil_kernel, chunk),
        out_shape=jax.ShapeDtypeStruct((rows, 2 * chunk), BF),
        grid=(rows // step,),
        in_specs=[spec(2 * chunk), spec(chunk), spec(chunk), spec(128), spec(128), pl.BlockSpec((8, 2 * chunk), lambda i: (0, 0))],
        out_specs=spec(2 * chunk),
        compiler_params=PARAMS,
        name="stencil",
        cost_estimate=pl.CostEstimate(flops=20 * rows * 2 * chunk, bytes_accessed=6 * rows * chunk * 2, transcendentals=0),
    )(flat(full), flat(up), flat(down), flat(north), flat(south), coeff)
    return out.reshape(full.shape)


def inner_products(core, half, y_ref, x_ref, mine, other):
    n = x_ref.shape[1]
    dot = lambda a, b: lax.dot_general(a, b, NT, preferred_element_type=F32)
    for out, which in ((mine, core), (other, 1 - core)):
        at = pl.multiple_of(which * half, half)
        re, im = y_ref[0, pl.ds(at, half), :], y_ref[1, pl.ds(at, half), :]
        out[:, :n] = dot(re, x_ref[0]) + dot(im, x_ref[1])
        out[:, n:] = dot(re, x_ref[1]) - dot(im, x_ref[0])


def hankel_kernel(nf, cols, *refs):
    parts, x_ref = refs[:nf], refs[nf]
    mine, other, full = refs[nf + 1 :]
    me = lax.axis_index("freq")
    core = lax.rem(lax.axis_index("space"), 2)
    for d in range(nf):
        at = pl.multiple_of(lax.rem(me + nf - d, nf) * cols, cols)
        for c in range(2):
            full[c, pl.ds(at, cols), :] = parts[d][c]
    inner_products(core, nf * cols // 2, full, x_ref, mine, other)


def image_kernel(y_ref, x_ref, mine, other):
    core = lax.rem(lax.axis_index("space"), 2)
    inner_products(core, y_ref.shape[1] // 2, y_ref, x_ref, mine, other)


def split(a):
    high = a.astype(BF)
    return high, (a - high.astype(F32)).astype(BF)


def product3(a, b_high, b_low, dims):
    high, low = split(a)
    dot = lambda u, v: lax.dot_general(u, v, dims, preferred_element_type=F32)
    return dot(high, b_high) + (dot(high, b_low) + dot(low, b_high))


def balance_kernel(n, h_ref, t_ref, m_ref, ph, plo, fh, flo, hh, hl, p_ref, p2_ref):
    step = 128
    h = h_ref[...]
    alpha = 2.0 / jnp.sum(h * h)
    high, low = split(h)
    hh[...], hl[...] = high, low
    fh[:n, :], flo[:n, :] = high, low
    fh[n:, :n], flo[n:, :n] = -high[:, n:], -low[:, n:]
    fh[n:, n:], flo[n:, n:] = high[:, :n], low[:, :n]

    @pl.loop(0, n // step)
    def _(i):
        rows = pl.ds(pl.multiple_of(i * step, step), step)
        a = alpha * h_ref[rows, :]
        re = product3(a, hh[...], hl[...], NT)
        im = product3(jnp.concatenate([a[:, n:], -a[:, :n]], 1), hh[...], hl[...], NT)
        p_ref[rows, :n] = re
        p_ref[rows, n:] = im

    p = p_ref[...]
    high, low = split(p)
    ph[:n, :], plo[:n, :] = high, low
    ph[n:, :n], plo[n:, :n] = -high[:, n:], -low[:, n:]
    ph[n:, n:], plo[n:, n:] = high[:, :n], low[:, :n]

    @pl.loop(0, n // step)
    def _(i):
        rows = pl.ds(pl.multiple_of(i * step, step), step)
        p2_ref[rows, :] = product3(p_ref[rows, :], ph[...], plo[...], NN)

    @pl.loop(0, n // step)
    def _(i):
        at = pl.multiple_of(i * step, step)
        rows = pl.ds(at, step)
        p2 = p2_ref[rows, :]
        p3 = product3(p2, ph[...], plo[...], NN)
        eye = lax.broadcasted_iota(jnp.int32, (step, 2 * n), 1) == at + lax.broadcasted_iota(jnp.int32, (step, 2 * n), 0)
        q = jnp.where(eye, 4.0, 0.0) - 6.0 * p_ref[rows, :] + 4.0 * p2 - p3
        t = product3(alpha * q, fh[...], flo[...], NN).astype(BF)
        t_ref[rows, :] = t
        m_ref[rows, :] = t
        m_ref[pl.ds(pl.multiple_of(n + at, step), step), :n] = -t[:, n:]
        m_ref[pl.ds(pl.multiple_of(n + at, step), step), n:] = t[:, :n]


def phi_kernel(nf, cols, m_ref, x_ref, *refs):
    outs, phi = refs[:nf], refs[nf]
    n = nf * cols
    me = lax.axis_index("freq")
    dot = lambda u, v: lax.dot_general(u, v, NN, preferred_element_type=F32)
    step = 256

    @pl.loop(0, 2 * n // step)
    def _(i):
        rows = pl.ds(pl.multiple_of(i * step, step), step)
        phi[rows, :] = (dot(m_ref[rows, :n], x_ref[0]) + dot(m_ref[rows, n:], x_ref[1])).astype(BF)

    for d in range(nf):
        dest = lax.rem(me + d, nf)
        for c in range(2):
            outs[d][c] = phi[pl.ds(pl.multiple_of(c * n + dest * cols, cols), cols), :]


def place_kernel(nf, chunk, *refs):
    parts, out = refs[:nf], refs[nf]
    me = lax.axis_index("freq")
    for d in range(nf):
        src = lax.rem(me + nf - d, nf)
        for p in range(2):
            at = pl.multiple_of(p * PLANE + src * chunk, chunk)
            out[:, :, pl.ds(at, chunk)] = parts[d][:, :, p * chunk : (p + 1) * chunk]


def core_swap(value, ns):
    return lax.ppermute(value, "space", [(i, i ^ 1) for i in range(ns)])


def chip_groups(ns):
    return [list(range(c, ns, 2)) for c in range(2)]


def scatter_sum(mine, other, nf, ns):
    chips = ns // 2
    part = mine + core_swap(other, ns)
    part = part.reshape(chips, part.shape[0] // chips, part.shape[1])
    part = lax.all_to_all(part, "space", 0, 0, tiled=True, axis_index_groups=chip_groups(ns))
    part = jnp.sum(part, 0)
    hop = 1
    while hop < nf:
        part = part + lax.ppermute(part, "freq", [(i, i ^ hop) for i in range(nf)])
        hop *= 2
    return part


def gather_rows(rows, ns):
    chips = ns // 2
    held = jnp.broadcast_to(rows[None], (chips,) + rows.shape)
    held = lax.all_to_all(held, "space", 0, 0, tiled=True, axis_index_groups=chip_groups(ns))
    held = held.reshape(chips * rows.shape[0], rows.shape[1])
    away = core_swap(held, ns)
    first = lax.rem(lax.axis_index("space"), 2) == 0
    return jnp.concatenate([jnp.where(first, held, away), jnp.where(first, away, held)], 0)


def coefficients(coupling, wall, chunk, nf):
    me = lax.axis_index("freq")
    pick = lambda v: lax.dynamic_slice_in_dim(v.reshape(-1, 2, nf, chunk), me, 1, 2).reshape(-1, 2 * chunk)
    mine, solid = pick(coupling), pick(wall[None]) == 1
    z = jnp.arange(2 * chunk, dtype=jnp.int32) % NZ
    keep = jnp.stack([z >= 0, z >= 0, z >= 0, z >= 0, z >= 0, z != NZ - 1, z != 0])
    held = jnp.array([1, 0, 0, 0, 0, 0, 0], F32)[:, None]
    coeff = jnp.where(solid, held, jnp.where(keep, mine, 0.0))
    return jnp.concatenate([coeff, jnp.zeros((1, 2 * chunk), F32)], 0)


def shards(nf, ns, direct, adjoint, coupling, wall):
    cols = direct.shape[1]
    n = nf * cols
    chunk = PLANE // nf
    coeff = coefficients(coupling, wall, chunk, nf)
    x_parts = rotate(spread(direct, nf), nf)
    sds = jax.ShapeDtypeStruct
    full, low, high, first, last = call(
        functools.partial(gather_kernel, nf, cols, chunk),
        [sds((2, n, 2 * chunk), BF)] + [sds((2, n, chunk), BF)] * 2 + [sds((2, n, 128), BF)] * 2,
        x_parts,
        "gather",
        moved=10 * n * chunk * 2,
    )
    y_parts = rotate(spread(adjoint, nf, after=x_parts[1:]), nf)
    ahead = [(i, i + 1) for i in range(ns - 1)]
    back = [(i + 1, i) for i in range(ns - 1)]
    up = lax.ppermute(low, "space", back)
    down = lax.ppermute(high, "space", ahead)
    north = lax.ppermute(first, "freq", [(i + 1, i) for i in range(nf - 1)])
    south = lax.ppermute(last, "freq", [(i, i + 1) for i in range(nf - 1)])
    image = stencil(full, up, down, north, south, coeff, chunk)
    halves = [sds((n // 2, 2 * n), F32)] * 2
    work = 8 * n * n * 2 * chunk
    mine, other, y_full = call(
        functools.partial(hankel_kernel, nf, cols),
        halves + [sds((2, n, 2 * chunk), BF)],
        (*y_parts, full),
        "hankel",
        flops=work,
        moved=10 * n * chunk * 2,
    )
    hank = gather_rows(scatter_sum(mine, other, nf, ns), ns)
    g_mine, g_other = call(image_kernel, halves, (y_full, image), "image", flops=work, moved=8 * n * chunk * 2)
    g_rows = scatter_sum(g_mine, g_other, nf, ns)
    vm = lambda dtype, rows: pltpu.VMEM((rows, 2 * n), dtype)
    table, mapping = call(
        functools.partial(balance_kernel, n),
        [sds((n, 2 * n), BF), sds((2 * n, 2 * n), BF)],
        (hank,),
        "balance",
        scratch=[vm(BF, 2 * n)] * 4 + [vm(BF, n)] * 2 + [vm(F32, n)] * 2,
        flops=96 * n * n * n,
        moved=10 * n * n,
    )
    phi_parts = call(
        functools.partial(phi_kernel, nf, cols),
        [sds((2, cols, 2 * chunk), BF)] * nf,
        (mapping, full),
        "phi",
        scratch=[pltpu.VMEM((2 * n, 2 * chunk), BF)],
        flops=work,
        moved=8 * n * chunk * 2,
    )
    got = rotate(phi_parts, nf)
    modes = call(functools.partial(place_kernel, nf, chunk), sds(direct.shape, BF), got, "place", moved=8 * n * chunk)
    wide = table.astype(F32)
    product = lambda a: lax.dot_general(a, wide, NT, precision=lax.Precision.HIGHEST)
    turned = jnp.concatenate([g_rows[:, n:], -g_rows[:, :n]], 1)
    rows = (n / 16.0) * jnp.concatenate([product(g_rows), product(turned)], 1)
    reduced = gather_rows(rows, ns)
    reduced = jnp.stack([reduced[:, :n], reduced[:, n:]], 0)
    return modes, reduced


def solution(mesh):
    return jax.shard_map(
        functools.partial(shards, mesh.shape["freq"], mesh.shape["space"]),
        mesh=mesh,
        in_specs=(P(None, "freq", "space"), P(None, "freq", "space"), P(None, "space"), P("space")),
        out_specs=(P(None, "freq", "space"), P()),
        check_vma=False,
    )
```
